512 devices in a mesh: freq: 64 (over y, z), tm: 2 (over x_lo), bl: 4 (over x_hi, core).
Axes of the slice: x: 4 (x_hi: 2, x_lo: 2; x = x_hi * 2 + x_lo), y: 4, z: 16, core: 2. Of those that a mesh axis runs over, the one named last changes fastest.
Arguments:
- samples: int32 [1024, 128, 2048], P(('freq', 'bl'), 'tm'), may hold values from 0 to 15
- chan_index: int32 [128], replicated, may hold values from 0 to 1023, as said below
Outputs:
- visibilities: float32 [128, 4, 2, 512, 512], P(('freq', 'tm'), 'bl')
The draws below stay inside these ranges and needn't reach their ends.
Inputs may be any that keep to these rules, and one draw needn't show every extreme that they name: `chan_index`: the entries are distinct.
All inputs are finite; a program needn't handle non-finite values.
Results may differ from the reference program's by a relative error of at most 0.0064.
Values may be sent and summed in bfloat16 or wider, within the bound.
A program may use at most 64 MiB of HBM per device.

```python
import math
import jax
import jax.numpy as jnp
from jax import lax

NIN = 1024
FRAME = 2048
TAPS = 4
CH = 128
FRAMES = 128


def draw_chan_index(key, part):
    half = FRAME // 2
    inner = jax.random.permutation(key, half - 2)[:CH - 2] + 1
    chosen = jnp.concatenate([inner.astype(jnp.int32), jnp.array([0, half - 1], jnp.int32)])
    order = jax.random.permutation(jax.random.fold_in(key, 7), CH)
    return chosen[order].astype(jnp.int32)


def place_ends(values, key, least, high):
    shape = values.shape
    spot = [jax.random.randint(jax.random.fold_in(key, axis), (), 0, shape[axis]) for axis in range(len(shape))]
    values = values.at[tuple(spot)].set(least)
    longest = shape.index(max(shape))
    spot[longest] = (spot[longest] + 1) % shape[longest]
    return values.at[tuple(spot)].set(high)


def setup_inputs(seed: int = 0) -> dict:
    streams_of = jax.random.split(jax.random.key(seed), 3)
    samples = place_ends(jax.random.randint(streams_of[0], (NIN, FRAMES, FRAME), 0, 16), jax.random.fold_in(streams_of[0], 1), 0, 15).astype(jnp.int32)
    chan_index = draw_chan_index(jax.random.fold_in(streams_of[2], 71), 0)
    return dict(samples=samples, chan_index=chan_index)


def tap_table(frame):
    place = jnp.arange(TAPS * frame, dtype=jnp.float32) + 0.5
    shifted = (place - 2.0 * frame) / frame
    window = 0.5 - 0.5 * jnp.cos(place * (2.0 * math.pi / (TAPS * frame)))
    return (jnp.sinc(shifted) * window).reshape(TAPS, frame)

def dft_table(chan_index, frame):
    steps = jnp.arange(frame, dtype=jnp.int32)
    phase = chan_index[None, :] * steps[:, None] % frame
    angle = phase.astype(jnp.float32) * (2.0 * math.pi / frame)
    scale = 1.0 / math.sqrt(frame)
    both = jnp.stack([jnp.cos(angle) * scale, -jnp.sin(angle) * scale], axis=-1)
    return both.reshape(frame, -1).astype(jnp.bfloat16)

def apply_taps(padded, taps):
    count = padded.shape[1] - (TAPS - 1)
    total = taps[0][None, None, :] * padded[:, 0:count]
    for k in range(1, TAPS):
        total = total + taps[k][None, None, :] * padded[:, k:k + count]
    return total

def reference(samples, chan_index):
    frame = FRAME
    taps = tap_table(frame)
    table = dft_table(chan_index, frame).astype(jnp.float32)
    blocks = samples.reshape(NIN // 16, 16, FRAMES, frame)

    def channelize(block):
        volts = (block.astype(jnp.float32) - 7.5) * 0.25
        zeros = jnp.zeros((16, TAPS - 1, frame), jnp.float32)
        padded = jnp.concatenate([zeros, volts], axis=1)
        filtered = apply_taps(padded, taps).astype(jnp.bfloat16)
        flat = filtered.reshape(16 * FRAMES, frame).astype(jnp.float32)
        spec = jnp.dot(flat, table, preferred_element_type=jnp.float32)
        return spec.astype(jnp.bfloat16).reshape(16, FRAMES, 2 * CH)
    spectra = lax.map(channelize, blocks).reshape(NIN, FRAMES, CH, 2)
    per_chan = jnp.transpose(spectra, (2, 3, 0, 1))
    half = NIN // 2

    def correlate(chan):
        real_part = chan[0].astype(jnp.float32)
        imag_part = chan[1].astype(jnp.float32)
        tiles = []
        for tile in range(4):
            row_block = tile // 2
            col_block = tile % 2
            rows_re = real_part[row_block * half:(row_block + 1) * half]
            rows_im = imag_part[row_block * half:(row_block + 1) * half]
            cols_re = real_part[col_block * half:(col_block + 1) * half]
            cols_im = imag_part[col_block * half:(col_block + 1) * half]
            right = jnp.concatenate([cols_re, cols_im], axis=1)
            left_re = jnp.concatenate([rows_re, rows_im], axis=1)
            left_im = jnp.concatenate([rows_im, -rows_re], axis=1)
            vis_re = jnp.dot(left_re, right.T, preferred_element_type=jnp.float32)
            vis_im = jnp.dot(left_im, right.T, preferred_element_type=jnp.float32)
            tiles.append(jnp.stack([vis_re, vis_im], axis=0) / FRAMES)
        return jnp.stack(tiles, axis=0)
    return lax.map(correlate, per_chan)
```

```python
import functools
import math

import jax
import jax.numpy as jnp
import numpy as np
from jax import lax
from jax.experimental import pallas as pl
from jax.experimental.pallas import tpu as pltpu
from jax.sharding import PartitionSpec as P

TAPS = 4
FRAME = 2048
NY, NZ, NX = 4, 16, 2
CHANS = NY * NZ * NX
LANES = 128
MESH = pl.DeviceIdType.MESH
OFFSETS = (0, 1, -1, 2, -2, 3, -3, 4, -4, 5, -5, 6, -6, 7, -7, 8)
WAVES = ((0, 8), (8, 16))


def tap_constants():
    place = np.arange(TAPS * FRAME, dtype=np.float64) + 0.5
    shifted = (place - 2.0 * FRAME) / FRAME
    window = 0.5 - 0.5 * np.cos(place * (2.0 * math.pi / (TAPS * FRAME)))
    return (np.sinc(shifted) * window).reshape(TAPS, FRAME).astype(np.float32)


def cos_sin(phase):
    quarter = FRAME // 4
    turn = (phase + quarter // 2) // quarter
    rest = (phase - turn * quarter).astype(jnp.float32) * (2.0 * math.pi / FRAME)
    sq = rest * rest
    sin = rest * (1.0 + sq * (-1.0 / 6 + sq * (1.0 / 120 + sq * (-1.0 / 5040 + sq * (1.0 / 362880)))))
    cos = 1.0 + sq * (-0.5 + sq * (1.0 / 24 + sq * (-1.0 / 720 + sq * (1.0 / 40320))))
    odd = turn % 2 == 1
    c = jnp.where(odd, sin, cos)
    s = jnp.where(odd, cos, sin)
    c = jnp.where((turn % 4 == 1) | (turn % 4 == 2), -c, c)
    s = jnp.where(turn % 4 >= 2, -s, s)
    return c, s


def taps_applied(ext, taps):
    prior = pltpu.roll(ext, 1, 0)
    early = taps[1:2] * ext + taps[0:1] * prior
    late = taps[3:4] * ext + taps[2:3] * prior
    return (late + pltpu.roll(early, 2, 0))[8:].astype(jnp.bfloat16)


def to_volts(samples):
    return (samples.astype(jnp.float32) - 7.5) * 0.25


def channelize_kernel(
    samples, chan_ref, taps_ref, turned,
    raw, filtered, table, spread, mine, held, edge_out, edge_in,
    load_sem, edge_sem, zsend, zrecv, psend, own_sem, precv,
):
    freq = lax.axis_index("freq")
    tm = lax.axis_index("tm")
    bl = lax.axis_index("bl")
    y, z = freq // NZ, freq % NZ
    half = y // 2

    loads = [pltpu.make_async_copy(samples.at[:, 56:64], raw.at[:, 56:64], load_sem.at[0])]
    for i in range(4):
        loads.append(pltpu.make_async_copy(samples.at[i, 0:56], raw.at[i, 0:56], load_sem.at[1 + i]))
    for copy in loads:
        copy.start()

    barrier = pltpu.get_barrier_semaphore()
    for d in range(1, NZ):
        pl.semaphore_signal(barrier, inc=1, device_id=(y * NZ + (z + d) % NZ, tm, bl), device_id_type=MESH)
    for n in range(1, 32):
        yo, xo, bo = n // 8, n // 4 % 2, n % 4
        peer = ((y + yo) % NY * NZ + z, (tm + xo) % NX, (bl + bo) % 4)
        pl.semaphore_signal(barrier, inc=1, device_id=peer, device_id_type=MESH)

    row = lax.broadcasted_iota(jnp.int32, (CHANS, LANES), 0)
    lane = lax.broadcasted_iota(jnp.int32, (CHANS, LANES), 1)
    source = (row // 2 % NY) * (NZ * NX) + row // 8 * NX + row % 2
    picked = jnp.where(lane == source, jnp.broadcast_to(chan_ref[...], (CHANS, LANES)), 0)
    chan = jnp.broadcast_to(jnp.sum(picked.astype(jnp.float32), axis=1, keepdims=True), (CHANS, LANES))
    chan = chan.astype(jnp.int32)
    scale = 1.0 / math.sqrt(FRAME)
    re, im = cos_sin(chan * lane % FRAME)
    parts = [(re * scale, -im * scale)]
    for step in (128, 256, 512, 1024):
        c, s = cos_sin(chan * step % FRAME)
        parts += [(a * c + b * s, b * c - a * s) for a, b in parts]
    for k, (a, b) in enumerate(parts):
        table[0:CHANS, k * LANES : (k + 1) * LANES] = a.astype(jnp.bfloat16)
        table[CHANS:, k * LANES : (k + 1) * LANES] = b.astype(jnp.bfloat16)

    loads[0].wait()
    edge_copy = pltpu.make_async_remote_copy(
        edge_out, edge_in, edge_sem.at[0], edge_sem.at[1],
        device_id=(freq, 1 - tm, bl), device_id_type=MESH,
    )
    for i in range(4):
        edge_out[4 * i : 4 * i + 4] = to_volts(raw[i, 60:64]).astype(jnp.bfloat16)
    pl.semaphore_wait(barrier, 46)

    @pl.when(tm == 0)
    def _():
        edge_copy.start()

    for i in range(4):
        loads[1 + i].wait()

        @pl.loop(0, FRAME // LANES)
        def _(k):
            cols = pl.ds(pl.multiple_of(k * LANES, LANES), LANES)
            filtered[i * 64 + 8 : i * 64 + 64, cols] = taps_applied(to_volts(raw[i, :, cols]), taps_ref[:, cols])

    @pl.when(tm == 0)
    def _():
        edge_in[...] = jnp.zeros_like(edge_in)
        edge_copy.wait_send()

    @pl.when(tm == 1)
    def _():
        edge_copy.wait_recv()

    @pl.loop(0, FRAME // LANES)
    def _(k):
        cols = pl.ds(pl.multiple_of(k * LANES, LANES), LANES)
        before = edge_in[:, cols].astype(jnp.float32)
        for i in range(4):
            ext = jnp.concatenate(
                [before[4 * i : 4 * i + 4], before[4 * i : 4 * i + 4], to_volts(raw[i, 0:8, cols])], axis=0
            )
            filtered[i * 64 : i * 64 + 8, cols] = taps_applied(ext, taps_ref[:, cols])

    spectra = lax.dot_general(
        table[...], filtered[...], (((1,), (1,)), ((), ())), preferred_element_type=jnp.float32
    )
    first = lane < 64
    for t in range(2):
        re = spectra[:CHANS, t * LANES : (t + 1) * LANES]
        im = spectra[CHANS:, t * LANES : (t + 1) * LANES]
        spread[pl.ds(2 * t, CHANS, stride=4), :] = jnp.where(first, re, pltpu.roll(im, 64, 1))
        spread[pl.ds(2 * t + 1, CHANS, stride=4), :] = jnp.where(first, pltpu.roll(re, 64, 1), im)
    mine[...] = spread[...].astype(jnp.bfloat16).reshape(NZ, NY * NX, 4, LANES)

    own = pltpu.make_async_copy(mine.at[z], held.at[0], zrecv.at[0])
    own.start()
    for slot in range(1, NZ):
        to = (z - OFFSETS[slot] + NZ) % NZ
        pltpu.make_async_remote_copy(
            mine.at[to], held.at[slot], zsend, zrecv.at[0 if slot < 8 else 1],
            device_id=(y * NZ + to, tm, bl), device_id_type=MESH,
        ).start()

    for w, (lo, hi) in enumerate(WAVES):
        pltpu.make_async_copy(held.at[lo:hi], held.at[lo:hi], zrecv.at[w]).wait()
        land = turned.at[tm, y, lo:hi, bl]
        for yo in range(NY):
            for xo in range(NX):
                y_to, x_to = (y + yo) % NY, (tm + xo) % NX
                block = held.at[lo:hi, y_to * NX + x_to]
                for j, to in enumerate((1, 2, 3 * half)):
                    remote = yo or xo
                    copy = pltpu.make_async_remote_copy(
                        block, land, psend.at[w] if remote else own_sem.at[w, j], precv.at[w],
                        device_id=(y_to * NZ + z, x_to, to), device_id_type=MESH,
                    )
                    if remote:
                        copy.start()
                        continue

                    @pl.when(to != bl)
                    def _():
                        copy.start()

                    @pl.when(to == bl)
                    def _():
                        pltpu.make_async_copy(block, land, precv.at[w]).start()

    for w, (lo, hi) in enumerate(WAVES):
        sent = spread.at[0 : 42 * (hi - lo)]
        pltpu.make_async_copy(sent, sent, psend.at[w]).wait()
        block = held.at[lo:hi, 0]
        for j, to in enumerate((1, 2, 3 * half)):

            @pl.when(to != bl)
            def _():
                pltpu.make_async_copy(block, block, own_sem.at[w, j]).wait()

        middle = (bl == 1) | (bl == 2)

        @pl.when(middle)
        def _():
            got = turned.at[:, :, lo:hi]
            pltpu.make_async_copy(got, got, precv.at[w]).wait()

        @pl.when(jnp.logical_not(middle))
        def _():
            got = turned.at[:, 0:2, lo:hi]
            pltpu.make_async_copy(got, got, precv.at[w]).wait()

    sent = mine.at[0 : NZ - 1]
    pltpu.make_async_copy(sent, sent, zsend).wait()


def correlate_kernel(turned, out, rows, turned_rows, cols):
    z = lax.axis_index("freq") % NZ
    bl = lax.axis_index("bl")
    sign = jnp.where(lax.broadcasted_iota(jnp.int32, (16, LANES), 1) < 64, 1.0, -1.0)

    @pl.when(pl.program_id(0) == 0)
    def _():
        for slot in range(NZ):
            at = (z + OFFSETS[slot] + NZ) % NZ * 16
            for yi in range(2):
                place = pl.ds(pl.multiple_of(at + yi * 256, 16), 16)
                for x in range(NX):
                    k = slice(x * LANES, (x + 1) * LANES)
                    block = turned[x, bl // 2 * 2 + yi, slot]
                    rows[place, k] = block
                    turned_rows[place, k] = (pltpu.roll(block.astype(jnp.float32), 64, 1) * sign).astype(jnp.bfloat16)
                    cols[place, k] = turned[x, bl % 2 * 2 + yi, slot]

    count = out.shape[3]
    part = pl.ds(pl.multiple_of(pl.program_id(0) * count, count), count)
    for p, left in enumerate((rows, turned_rows)):
        product = lax.dot_general(
            left[part], cols[...], (((1,), (1,)), ((), ())), preferred_element_type=jnp.float32
        )
        out[0, 0, p] = product * (1.0 / 128)


def on_device(samples, chan_index):
    bf16, f32 = jnp.bfloat16, jnp.float32
    vmem = pl.BlockSpec(memory_space=pltpu.VMEM)
    anywhere = pl.BlockSpec(memory_space=pl.ANY)
    dma = pltpu.SemaphoreType.DMA
    turned = pl.pallas_call(
        channelize_kernel,
        out_shape=jax.ShapeDtypeStruct((NX, NY, NZ, 4, 4, LANES), bf16),
        in_specs=[anywhere, vmem, vmem],
        out_specs=anywhere,
        scratch_shapes=[
            pltpu.VMEM((4, 64, FRAME), jnp.int32),
            pltpu.VMEM((256, FRAME), bf16),
            pltpu.VMEM((2 * CHANS, FRAME), bf16),
            pltpu.VMEM((4 * CHANS, LANES), f32),
            pltpu.VMEM((NZ, NY * NX, 4, LANES), bf16),
            pltpu.VMEM((NZ, NY * NX, 4, LANES), bf16),
            pltpu.VMEM((16, FRAME), bf16),
            pltpu.VMEM((16, FRAME), bf16),
            dma((5,)),
            dma((2,)),
            dma,
            dma((2,)),
            dma((2,)),
            dma((2, 3)),
            dma((2,)),
        ],
        compiler_params=pltpu.CompilerParams(
            collective_id=0, has_side_effects=True, vmem_limit_bytes=40 * 2**20
        ),
        name="channelize",
    )(samples, chan_index.reshape(1, CHANS), jnp.asarray(tap_constants()))
    turned = turned.reshape(NX, NY, NZ, 16, LANES)
    steps = 4
    return pl.pallas_call(
        correlate_kernel,
        out_shape=jax.ShapeDtypeStruct((1, 1, 2, 512, 512), f32),
        grid=(steps,),
        in_specs=[vmem],
        out_specs=pl.BlockSpec((1, 1, 2, 512 // steps, 512), lambda i: (0, 0, 0, i, 0)),
        scratch_shapes=[pltpu.VMEM((512, 256), bf16)] * 3,
        compiler_params=pltpu.CompilerParams(vmem_limit_bytes=40 * 2**20),
        name="correlate",
    )(turned)


def solution(mesh):
    placed = (P(("freq", "bl"), "tm", None), P())
    return jax.shard_map(
        on_device,
        mesh=mesh,
        in_specs=placed,
        out_specs=P(("freq", "tm"), "bl", None, None, None),
        check_vma=False,
    )
```

```python
import math

import jax
import jax.numpy as jnp
import numpy as np
from jax import lax
from jax.experimental import pallas as pl
from jax.experimental.pallas import tpu as pltpu
from jax.sharding import PartitionSpec as P

TAPS = 4
FRAME = 2048
NY, NZ, NX = 4, 16, 2
CHANS = NY * NZ * NX
LANES = 128
MESH = pl.DeviceIdType.MESH
WAVES = ((0, 8), (8, 16))
VMEM_LIMIT = 58 * 2**20
STEPS = 4


def tap_constants():
    place = np.arange(TAPS * FRAME, dtype=np.float64) + 0.5
    shifted = (place - 2.0 * FRAME) / FRAME
    window = 0.5 - 0.5 * np.cos(place * (2.0 * math.pi / (TAPS * FRAME)))
    return (np.sinc(shifted) * window).reshape(TAPS, FRAME).astype(np.float32)


def cos_sin(phase):
    turn = (phase + FRAME // 8) >> 9
    rest = (phase - (turn << 9)).astype(jnp.float32) * (2.0 * math.pi / FRAME)
    sq = rest * rest
    sin = rest * (1.0 + sq * (-1.0 / 6 + sq * (1.0 / 120 + sq * (-1.0 / 5040 + sq * (1.0 / 362880)))))
    cos = 1.0 + sq * (-0.5 + sq * (1.0 / 24 + sq * (-1.0 / 720 + sq * (1.0 / 40320))))
    odd = (turn & 1) == 1
    c = jnp.where(odd, sin, cos)
    s = jnp.where(odd, cos, sin)
    c = jnp.where(((turn + 1) & 2) == 2, -c, c)
    s = jnp.where((turn & 2) == 2, -s, s)
    return c, s


def taps_applied(ext, taps):
    prior = pltpu.roll(ext, 1, 0)
    early = taps[1:2] * ext + taps[0:1] * prior
    late = taps[3:4] * ext + taps[2:3] * prior
    return (late + pltpu.roll(early, 2, 0))[8:].astype(jnp.bfloat16)


def to_volts(samples):
    return (samples.astype(jnp.float32) - 7.5) * 0.25


def make_table(chan_ref, table):
    rows = 16
    lane = lax.broadcasted_iota(jnp.int32, (rows, LANES), 1)
    scale = 1.0 / math.sqrt(FRAME)

    @pl.loop(0, CHANS // rows)
    def _(block):
        row = lax.broadcasted_iota(jnp.int32, (rows, LANES), 0) + block * rows
        source = ((row >> 1) & 3) * (NZ * NX) + (row >> 3) * NX + (row & 1)
        picked = jnp.where(lane == source, jnp.broadcast_to(chan_ref[...], (rows, LANES)), 0)
        chan = jnp.sum(picked.astype(jnp.float32), axis=1, keepdims=True)
        chan = jnp.broadcast_to(chan, (rows, LANES)).astype(jnp.int32)
        re, im = cos_sin((chan * lane) & (FRAME - 1))
        parts = [(re * scale, -im * scale)]
        for step in (128, 256):
            c, s = cos_sin((chan * step) & (FRAME - 1))
            parts += [(a * c + b * s, b * c - a * s) for a, b in parts]
        quarter = chan & 3
        c = jnp.where(quarter == 0, 1.0, jnp.where(quarter == 2, -1.0, 0.0))
        s = jnp.where(quarter == 1, 1.0, jnp.where(quarter == 3, -1.0, 0.0))
        parts += [(a * c + b * s, b * c - a * s) for a, b in parts]
        sign = (1 - 2 * (chan & 1)).astype(jnp.float32)
        parts += [(a * sign, b * sign) for a, b in parts]
        at = pl.multiple_of(block * rows, rows)
        for k, (a, b) in enumerate(parts):
            table[pl.ds(at, rows), k * LANES : (k + 1) * LANES] = a.astype(jnp.bfloat16)
            table[pl.ds(at + CHANS, rows), k * LANES : (k + 1) * LANES] = b.astype(jnp.bfloat16)


def channelize_kernel(
    samples, chan_hbm, taps_hbm, turned,
    raw, chan_ref, taps_ref, filtered, table, spread, mine, held, edge_out, edge_in,
    load_sem, edge_sem, zsend, zrecv, psend, own_sem, precv, in_sem, plane_sem,
):
    freq = lax.axis_index("freq")
    tm = lax.axis_index("tm")
    bl = lax.axis_index("bl")
    y, z = freq // NZ, freq % NZ
    half = y // 2

    loads = [
        pltpu.make_async_copy(chan_hbm, chan_ref, load_sem.at[5]),
        pltpu.make_async_copy(samples.at[:, 56:64], raw.at[:, 56:64], load_sem.at[0]),
        pltpu.make_async_copy(taps_hbm, taps_ref, load_sem.at[6]),
    ]
    for i in range(4):
        loads.append(pltpu.make_async_copy(samples.at[i, 0:56], raw.at[i, 0:56], load_sem.at[1 + i]))
    for copy in loads:
        copy.start()

    barrier = pltpu.get_barrier_semaphore()
    partner = (freq, 1 - tm, bl)

    @pl.when(tm == 1)
    def _():
        pl.semaphore_signal(barrier, inc=1, device_id=partner, device_id_type=MESH)

    @pl.loop(z + 1, NZ)
    def _(t):
        pl.semaphore_signal(barrier, inc=1, device_id=(y * NZ + t, tm, bl), device_id_type=MESH)

    for n in range(15, -1, -1):
        peer = ((y + n // 4) % NY * NZ + z, 1, (bl + n) % 4)
        if n:
            pl.semaphore_signal(barrier, inc=1, device_id=peer, device_id_type=MESH)
            continue

        @pl.when(tm == 0)
        def _():
            pl.semaphore_signal(barrier, inc=1, device_id=peer, device_id_type=MESH)

    loads[0].wait()
    make_table(chan_ref, table)

    loads[1].wait()
    edge_copy = pltpu.make_async_remote_copy(
        edge_out, edge_in, edge_sem.at[0], edge_sem.at[1], device_id=partner, device_id_type=MESH
    )
    for i in range(4):
        edge_out[4 * i : 4 * i + 4] = to_volts(raw[i, 60:64]).astype(jnp.bfloat16)
    loads[2].wait()

    @pl.when(tm == 0)
    def _():
        pl.semaphore_wait(barrier, z + 1)
        edge_copy.start()

    for i in range(4):
        loads[3 + i].wait()

        @pl.loop(0, FRAME // LANES)
        def _(k):
            cols = pl.ds(pl.multiple_of(k * LANES, LANES), LANES)
            filtered[i * 64 + 8 : i * 64 + 64, cols] = taps_applied(to_volts(raw[i, :, cols]), taps_ref[:, cols])

    @pl.when(tm == 0)
    def _():
        edge_in[...] = jnp.zeros_like(edge_in)
        edge_copy.wait_send()

    @pl.when(tm == 1)
    def _():
        pl.semaphore_wait(barrier, z + 31)
        pl.semaphore_signal(plane_sem, inc=1, device_id=partner, device_id_type=MESH)
        edge_copy.wait_recv()

    @pl.loop(0, z)
    def _(t):
        pl.semaphore_signal(in_sem.at[z], inc=1, device_id=(y * NZ + t, tm, bl), device_id_type=MESH)

    @pl.loop(0, FRAME // LANES)
    def _(k):
        cols = pl.ds(pl.multiple_of(k * LANES, LANES), LANES)
        before = edge_in[:, cols].astype(jnp.float32)
        for i in range(4):
            ext = jnp.concatenate(
                [before[4 * i : 4 * i + 4], before[4 * i : 4 * i + 4], to_volts(raw[i, 0:8, cols])], axis=0
            )
            filtered[i * 64 : i * 64 + 8, cols] = taps_applied(ext, taps_ref[:, cols])

    spectra = lax.dot_general(
        table[...], filtered[...], (((1,), (1,)), ((), ())), preferred_element_type=jnp.float32
    )
    first = lax.broadcasted_iota(jnp.int32, (CHANS, LANES), 1) < 64
    for t in range(2):
        re = spectra[:CHANS, t * LANES : (t + 1) * LANES]
        im = spectra[CHANS:, t * LANES : (t + 1) * LANES]
        spread[pl.ds(2 * t, CHANS, stride=4), :] = jnp.where(first, re, pltpu.roll(im, 64, 1))
        spread[pl.ds(2 * t + 1, CHANS, stride=4), :] = jnp.where(first, pltpu.roll(re, 64, 1), im)
    mine[...] = spread[...].astype(jnp.bfloat16).reshape(NZ, NY * NX, 4, LANES)

    wave = z // 8

    def send_along(t):
        pltpu.make_async_remote_copy(
            mine.at[t], held.at[z], zsend, zrecv.at[wave],
            device_id=(y * NZ + t, tm, bl), device_id_type=MESH,
        ).start()

    @pl.loop(0, z)
    def _(t):
        send_along(t)

    pltpu.make_async_copy(mine.at[z], held.at[z], zrecv.at[wave]).start()

    @pl.loop(z + 1, NZ)
    def _(t):
        pl.semaphore_wait(in_sem.at[t], 1)
        send_along(t)

    @pl.when(tm == 0)
    def _():
        pl.semaphore_wait(plane_sem, 1)

    for w, (lo, hi) in enumerate(WAVES):
        pltpu.make_async_copy(held.at[lo:hi], held.at[lo:hi], zrecv.at[w]).wait()
        land = turned.at[tm, y, lo:hi, bl]
        for yo in (2, 1, 3, 0):
            for xo in (1, 0):
                y_to, x_to = (y + yo) % NY, (tm + xo) % NX
                block = held.at[lo:hi, y_to * NX + x_to]
                for j, to in enumerate((1, 2, 3 * half)):
                    remote = yo or xo
                    copy = pltpu.make_async_remote_copy(
                        block, land, psend.at[w] if remote else own_sem.at[w, j], precv.at[w],
                        device_id=(y_to * NZ + z, x_to, to), device_id_type=MESH,
                    )
                    if remote:
                        copy.start()
                        continue

                    @pl.when(to != bl)
                    def _():
                        copy.start()

                    @pl.when(to == bl)
                    def _():
                        pltpu.make_async_copy(block, land, precv.at[w]).start()

    for w, (lo, hi) in enumerate(WAVES):
        sent = spread.at[0 : 42 * (hi - lo)]
        pltpu.make_async_copy(sent, sent, psend.at[w]).wait()
        block = held.at[lo:hi, 0]
        for j, to in enumerate((1, 2, 3 * half)):

            @pl.when(to != bl)
            def _():
                pltpu.make_async_copy(block, block, own_sem.at[w, j]).wait()

        middle = (bl == 1) | (bl == 2)

        @pl.when(middle)
        def _():
            got = turned.at[:, :, lo:hi]
            pltpu.make_async_copy(got, got, precv.at[w]).wait()

        @pl.when(jnp.logical_not(middle))
        def _():
            got = turned.at[:, 0:2, lo:hi]
            pltpu.make_async_copy(got, got, precv.at[w]).wait()

    sent = mine.at[0 : NZ - 1]
    pltpu.make_async_copy(sent, sent, zsend).wait()


def correlate_kernel(turned_hbm, out, turned, made, load_sem, sems):
    bl = lax.axis_index("bl")
    load = pltpu.make_async_copy(turned_hbm, turned, load_sem)
    load.start()
    load.wait()
    sign = jnp.where(lax.broadcasted_iota(jnp.int32, (1, LANES), 1) < 64, 1.0, -1.0)
    right = pl.ds(pl.multiple_of(bl % 2 * 512, 512), 512)
    cols = jnp.concatenate([turned[0, right], turned[1, right]], axis=1)
    count = 512 // STEPS
    copies = []
    for step in range(STEPS):
        part = pl.ds(pl.multiple_of(bl // 2 * 512 + step * count, count), count)
        halves = [turned[x, part] for x in range(NX)]
        turned_halves = [(pltpu.roll(h.astype(jnp.float32), 64, 1) * sign).astype(jnp.bfloat16) for h in halves]
        left = jnp.concatenate([jnp.concatenate(h, axis=1) for h in (halves, turned_halves)], axis=0)
        product = lax.dot_general(left, cols, (((1,), (1,)), ((), ())), preferred_element_type=jnp.float32)
        place = slice(step * count, (step + 1) * count)
        for p in range(2):
            made[0, 0, p, place] = product[p * count : (p + 1) * count] * (1.0 / 128)
        copies.append(pltpu.make_async_copy(made.at[:, :, :, place], out.at[:, :, :, place], sems.at[step]))
        copies[-1].start()
    for copy in copies:
        copy.wait()


def on_device(samples, chan_index):
    bf16, f32 = jnp.bfloat16, jnp.float32
    hbm = pl.BlockSpec(memory_space=pltpu.MemorySpace.HBM)
    dma = pltpu.SemaphoreType.DMA
    turned = pl.pallas_call(
        channelize_kernel,
        out_shape=jax.ShapeDtypeStruct((NX, NY, NZ, 4, 4, LANES), bf16),
        in_specs=[hbm, hbm, hbm],
        out_specs=pl.BlockSpec(memory_space=pl.ANY),
        scratch_shapes=[
            pltpu.VMEM((4, 64, FRAME), jnp.int32),
            pltpu.VMEM((1, CHANS), jnp.int32),
            pltpu.VMEM((TAPS, FRAME), f32),
            pltpu.VMEM((256, FRAME), bf16),
            pltpu.VMEM((2 * CHANS, FRAME), bf16),
            pltpu.VMEM((4 * CHANS, LANES), f32),
            pltpu.VMEM((NZ, NY * NX, 4, LANES), bf16),
            pltpu.VMEM((NZ, NY * NX, 4, LANES), bf16),
            pltpu.VMEM((16, FRAME), bf16),
            pltpu.VMEM((16, FRAME), bf16),
            dma((7,)),
            dma((2,)),
            dma,
            dma((2,)),
            dma((2,)),
            dma((2, 3)),
            dma((2,)),
            pltpu.SemaphoreType.REGULAR((NZ,)),
            pltpu.SemaphoreType.REGULAR,
        ],
        compiler_params=pltpu.CompilerParams(
            collective_id=0, has_side_effects=True, vmem_limit_bytes=VMEM_LIMIT
        ),
        name="channelize",
    )(samples, chan_index.reshape(1, CHANS), jnp.asarray(tap_constants()))
    turned = turned.reshape(NX, NY * NZ * 16, LANES)
    return pl.pallas_call(
        correlate_kernel,
        out_shape=jax.ShapeDtypeStruct((1, 1, 2, 512, 512), f32),
        in_specs=[hbm],
        out_specs=hbm,
        scratch_shapes=[
            pltpu.VMEM((NX, NY * NZ * 16, LANES), bf16),
            pltpu.VMEM((1, 1, 2, 512, 512), f32),
            dma,
            dma((STEPS,)),
        ],
        compiler_params=pltpu.CompilerParams(vmem_limit_bytes=VMEM_LIMIT),
        name="correlate",
    )(turned)


def solution(mesh):
    placed = (P(("freq", "bl"), "tm", None), P())
    return jax.shard_map(
        on_device,
        mesh=mesh,
        in_specs=placed,
        out_specs=P(("freq", "tm"), "bl", None, None, None),
        check_vma=False,
    )
```

```python
import math

import jax
import jax.numpy as jnp
import numpy as np
from jax import lax
from jax.experimental import pallas as pl
from jax.experimental.pallas import tpu as pltpu
from jax.sharding import PartitionSpec as P

TAPS = 4
FRAME = 2048
NY, NZ, NX = 4, 16, 2
CHANS = NY * NZ * NX
LANES = 128
MESH = pl.DeviceIdType.MESH
OFFSETS = (0, 1, -1, 2, -2, 3, -3, 4, -4, 5, -5, 6, -6, 7, -7, 8)
WAVES = ((0, 7), (7, 11), (11, 15), (15, 16))
EARLY = NZ // 2
HUB_Z = 11
VMEM_LIMIT = 40 * 2**20
UNROLL = 4
STEPS = 4


def tap_constants():
    place = np.arange(TAPS * FRAME, dtype=np.float64) + 0.5
    shifted = (place - 2.0 * FRAME) / FRAME
    window = 0.5 - 0.5 * np.cos(place * (2.0 * math.pi / (TAPS * FRAME)))
    taps = (np.sinc(shifted) * window).reshape(TAPS, FRAME).astype(np.float32)
    return taps * np.float32(0.25)


def cos_sin(phase):
    turn = (phase + FRAME // 8) >> 9
    rest = (phase - (turn << 9)).astype(jnp.float32) * (2.0 * math.pi / FRAME)
    sq = rest * rest
    sin = rest * (1.0 + sq * (-1.0 / 6 + sq * (1.0 / 120 + sq * (-1.0 / 5040 + sq * (1.0 / 362880)))))
    cos = 1.0 + sq * (-0.5 + sq * (1.0 / 24 + sq * (-1.0 / 720 + sq * (1.0 / 40320))))
    odd = (turn & 1) == 1
    c = jnp.where(odd, sin, cos)
    s = jnp.where(odd, cos, sin)
    c = jnp.where(((turn + 1) & 2) == 2, -c, c)
    s = jnp.where((turn & 2) == 2, -s, s)
    return c, s


def taps_applied(ext, taps):
    prior = pltpu.roll(ext, 1, 0)
    early = taps[1:2] * ext + taps[0:1] * prior
    late = taps[3:4] * ext + taps[2:3] * prior
    return (late + pltpu.roll(early, 2, 0))[8:].astype(jnp.bfloat16)


def centred(samples):
    return samples.astype(jnp.float32) - 7.5


def make_table(chan_ref, table, lo, hi):
    rows = 16
    lane = lax.broadcasted_iota(jnp.int32, (rows, LANES), 1)
    scale = 1.0 / math.sqrt(FRAME)

    @pl.loop(lo, hi, unroll=2)
    def _(block):
        row = lax.broadcasted_iota(jnp.int32, (rows, LANES), 0) + block * rows
        source = ((row >> 1) & 3) * (NZ * NX) + (row >> 3) * NX + (row & 1)
        picked = jnp.where(lane == source, jnp.broadcast_to(chan_ref[...], (rows, LANES)), 0)
        chan = jnp.sum(picked.astype(jnp.float32), axis=1, keepdims=True)
        chan = jnp.broadcast_to(chan, (rows, LANES)).astype(jnp.int32)
        re, im = cos_sin((chan * lane) & (FRAME - 1))
        parts = [(re * scale, -im * scale)]
        for step in (128, 256):
            c, s = cos_sin((chan * step) & (FRAME - 1))
            parts += [(a * c + b * s, b * c - a * s) for a, b in parts]
        quarter = chan & 3
        c = jnp.where(quarter == 0, 1.0, jnp.where(quarter == 2, -1.0, 0.0))
        s = jnp.where(quarter == 1, 1.0, jnp.where(quarter == 3, -1.0, 0.0))
        parts += [(a * c + b * s, b * c - a * s) for a, b in parts]
        sign = (1 - 2 * (chan & 1)).astype(jnp.float32)
        parts += [(a * sign, b * sign) for a, b in parts]
        at = pl.multiple_of(block * rows, rows)
        for k, (a, b) in enumerate(parts):
            table[pl.ds(at, rows), k * LANES : (k + 1) * LANES] = a.astype(jnp.bfloat16)
            table[pl.ds(at + CHANS, rows), k * LANES : (k + 1) * LANES] = b.astype(jnp.bfloat16)


def channelize_kernel(
    samples, chan_hbm, taps_hbm, turned,
    raw, chan_ref, taps_ref, filtered, table, spread, mine, held, edge_out, edge_in,
    load_sem, edge_sem, zsend, zrecv, psend, precv, in_sem, plane_sem, late_sem,
):
    freq = lax.axis_index("freq")
    tm = lax.axis_index("tm")
    bl = lax.axis_index("bl")
    y, z = freq // NZ, freq % NZ
    half = y // 2

    barrier = pltpu.get_barrier_semaphore()
    partner = (freq, 1 - tm, bl)
    early = z < EARLY
    along_hub = z == HUB_Z
    plane_hub = (y == 2) & (tm == 1) & (bl == 0)
    hub = along_hub | plane_hub

    def signal(sem, device):
        pl.semaphore_signal(sem, inc=1, device_id=device, device_id_type=MESH)

    def along(t):
        return (y * NZ + t, tm, bl)

    signal(barrier, partner)

    loads = [
        pltpu.make_async_copy(samples.at[:, 56:64], raw.at[:, 56:64], load_sem.at[0]),
        pltpu.make_async_copy(chan_hbm, chan_ref, load_sem.at[5]),
        pltpu.make_async_copy(taps_hbm, taps_ref, load_sem.at[6]),
    ]
    for i in range(4):
        loads.append(pltpu.make_async_copy(samples.at[i, 0:56], raw.at[i, 0:56], load_sem.at[1 + i]))
    for copy in loads:
        copy.start()

    @pl.when(early)
    def _():
        @pl.loop(z + 1, NZ)
        def _(t):
            signal(barrier, along(t))

    @pl.when(jnp.logical_not(early | along_hub))
    def _():
        signal(barrier, along(HUB_Z))

    @pl.when(jnp.logical_not(plane_hub))
    def _():
        signal(barrier, (2 * NZ + z, 1, 0))

    contacts = jnp.where(early, z, jnp.where(along_hub, NZ - 1, EARLY))
    contacts += jnp.where(plane_hub, 32, 1)

    loads[0].wait()
    edge_copy = pltpu.make_async_remote_copy(
        edge_out, edge_in, edge_sem.at[0], edge_sem.at[1], device_id=partner, device_id_type=MESH
    )
    for f in range(TAPS - 1):
        last = [raw[i, 64 - (TAPS - 1) + f : 65 - (TAPS - 1) + f] for i in range(4)]
        edge_out[f] = centred(jnp.concatenate(last, axis=0)).astype(jnp.bfloat16)
    loads[1].wait()
    make_table(chan_ref, table, 0, 4)

    def pass_on():
        @pl.when(along_hub)
        def _():
            for t in range(EARLY, NZ):
                if t != HUB_Z:
                    signal(late_sem, along(t))

        @pl.when(plane_hub)
        def _():
            for n in range(31, 0, -1):
                signal(plane_sem, ((y + n // 8) % NY * NZ + z, (tm + n // 4) % NX, (bl + n) % 4))

    def meet():
        pl.semaphore_wait(barrier, contacts)

        @pl.when(tm == 0)
        def _():
            edge_copy.start()

        @pl.loop(0, jnp.where(early, z, EARLY))
        def _(t):
            signal(in_sem.at[z], along(t))

        pass_on()

    @pl.when(jnp.logical_not(hub))
    def _():
        meet()

    make_table(chan_ref, table, 4, 8)
    loads[2].wait()

    for i in range(4):
        loads[3 + i].wait()

        @pl.loop(0, FRAME // LANES, unroll=UNROLL)
        def _(k):
            cols = pl.ds(pl.multiple_of(k * LANES, LANES), LANES)
            filtered[i * 64 + 8 : i * 64 + 64, cols] = taps_applied(centred(raw[i, :, cols]), taps_ref[:, cols])

    @pl.when(hub)
    def _():
        meet()

    @pl.when(tm == 0)
    def _():
        edge_in[...] = jnp.zeros_like(edge_in)
        edge_copy.wait_send()

    @pl.when(tm == 1)
    def _():
        edge_copy.wait_recv()

    @pl.loop(0, FRAME // LANES, unroll=2)
    def _(k):
        cols = pl.ds(pl.multiple_of(k * LANES, LANES), LANES)
        before = [edge_in[f, :, cols].astype(jnp.float32) for f in range(TAPS - 1)]
        for i in range(4):
            past = [before[f][i : i + 1] for f in (0, 0, 0, 0, 0, 0, 1, 2)]
            ext = jnp.concatenate(past + [centred(raw[i, 0:8, cols])], axis=0)
            filtered[i * 64 : i * 64 + 8, cols] = taps_applied(ext, taps_ref[:, cols])

    spectra = lax.dot_general(
        table[...], filtered[...], (((1,), (1,)), ((), ())), preferred_element_type=jnp.float32
    )
    first = lax.broadcasted_iota(jnp.int32, (CHANS, LANES), 1) < 64
    for t in range(2):
        re = spectra[:CHANS, t * LANES : (t + 1) * LANES]
        im = spectra[CHANS:, t * LANES : (t + 1) * LANES]
        spread[pl.ds(2 * t, CHANS, stride=4), :] = jnp.where(first, re, pltpu.roll(im, 64, 1))
        spread[pl.ds(2 * t + 1, CHANS, stride=4), :] = jnp.where(first, pltpu.roll(re, 64, 1), im)
    mine[...] = spread[...].astype(jnp.bfloat16).reshape(NZ, NY * NX, 4, LANES)

    def send_along(t):
        d = (z - t + 7 + NZ) % NZ - 7
        slot = jnp.where(d > 0, 2 * d - 1, -2 * d)
        wave = sum((slot >= lo).astype(jnp.int32) for lo, _ in WAVES[1:])
        pltpu.make_async_remote_copy(
            mine.at[t], held.at[slot], zsend, zrecv.at[wave], device_id=along(t), device_id_type=MESH
        ).start()

    pltpu.make_async_copy(mine.at[z], held.at[0], zrecv.at[0]).start()

    @pl.when(early)
    def _():
        @pl.loop(0, z)
        def _(t):
            send_along(t)

        @pl.loop(z + 1, NZ)
        def _(t):
            pl.semaphore_wait(in_sem.at[t], 1)
            send_along(t)

    @pl.when(jnp.logical_not(early))
    def _():
        @pl.loop(0, EARLY)
        def _(t):
            send_along(t)

        @pl.when(jnp.logical_not(along_hub))
        def _():
            pl.semaphore_wait(late_sem, 1)

        @pl.loop(EARLY, z)
        def _(t):
            send_along(t)

        @pl.loop(z + 1, NZ)
        def _(t):
            send_along(t)

    @pl.when(jnp.logical_not(plane_hub))
    def _():
        pl.semaphore_wait(plane_sem, 1)

    for w, (lo, hi) in enumerate(WAVES):
        pltpu.make_async_copy(held.at[lo:hi], held.at[lo:hi], zrecv.at[w]).wait()
        land = turned.at[tm, y, lo:hi, bl]
        for y_to in range(NY):
            for x_to in range(NX):
                block = held.at[lo:hi, y_to * NX + x_to]
                for to in (1, 3 * half, 2):
                    here = (y_to == y) & (x_to == tm) & (to == bl)

                    @pl.when(jnp.logical_not(here))
                    def _():
                        pltpu.make_async_remote_copy(
                            block, land, psend.at[w], precv.at[w],
                            device_id=(y_to * NZ + z, x_to, to), device_id_type=MESH,
                        ).start()

                    @pl.when(here)
                    def _():
                        pltpu.make_async_copy(block, land, precv.at[w]).start()

    middle = (bl == 1) | (bl == 2)
    to_self = middle | (bl == 3 * half)
    for w, (lo, hi) in enumerate(WAVES):

        @pl.when(to_self)
        def _():
            sent = spread.at[0 : 46 * (hi - lo)]
            pltpu.make_async_copy(sent, sent, psend.at[w]).wait()

        @pl.when(jnp.logical_not(to_self))
        def _():
            sent = spread.at[0 : 48 * (hi - lo)]
            pltpu.make_async_copy(sent, sent, psend.at[w]).wait()

        @pl.when(middle)
        def _():
            got = turned.at[:, :, lo:hi]
            pltpu.make_async_copy(got, got, precv.at[w]).wait()

        @pl.when(jnp.logical_not(middle))
        def _():
            got = turned.at[:, 0:2, lo:hi]
            pltpu.make_async_copy(got, got, precv.at[w]).wait()

    sent = mine.at[0 : NZ - 1]
    pltpu.make_async_copy(sent, sent, zsend).wait()


def correlate_kernel(turned, out, made, sems):
    z = lax.axis_index("freq") % NZ
    bl = lax.axis_index("bl")

    def rows(half, first, count):
        parts = []
        for n in range(first, first + count // 16):
            d = (n % NZ - z + 7 + NZ) % NZ - 7
            slot = jnp.where(d > 0, 2 * d - 1, -2 * d)
            parts.append([turned[x, half * 2 + n // NZ, slot] for x in range(NX)])
        return [jnp.concatenate(p, axis=0) for p in zip(*parts)]

    sign = jnp.where(lax.broadcasted_iota(jnp.int32, (1, LANES), 1) < 64, 1.0, -1.0)
    cols = jnp.concatenate(rows(bl % 2, 0, 512), axis=1)
    count = 512 // STEPS
    copies = []
    for step in range(STEPS):
        halves = rows(bl // 2, step * count // 16, count)
        turned_halves = [(pltpu.roll(h.astype(jnp.float32), 64, 1) * sign).astype(jnp.bfloat16) for h in halves]
        left = jnp.concatenate([jnp.concatenate(h, axis=1) for h in (halves, turned_halves)], axis=0)
        product = lax.dot_general(left, cols, (((1,), (1,)), ((), ())), preferred_element_type=jnp.float32)
        place = slice(step * count, (step + 1) * count)
        for p in range(2):
            made[0, 0, p, place] = product[p * count : (p + 1) * count] * (1.0 / 128)
        copies.append(pltpu.make_async_copy(made.at[:, :, :, place], out.at[:, :, :, place], sems.at[step]))
        copies[-1].start()
    for copy in copies:
        copy.wait()


def on_device(samples, chan_index):
    bf16, f32 = jnp.bfloat16, jnp.float32
    hbm = pl.BlockSpec(memory_space=pltpu.MemorySpace.HBM)
    dma = pltpu.SemaphoreType.DMA
    inputs = (samples, chan_index.reshape(1, CHANS), jnp.asarray(tap_constants()))
    turned = pl.pallas_call(
        channelize_kernel,
        out_shape=jax.ShapeDtypeStruct((NX, NY, NZ, 4, 4, LANES), bf16),
        in_specs=[hbm, hbm, hbm],
        out_specs=pl.BlockSpec(memory_space=pl.ANY),
        scratch_shapes=[
            pltpu.VMEM((4, 64, FRAME), jnp.int32),
            pltpu.VMEM((1, CHANS), jnp.int32),
            pltpu.VMEM((TAPS, FRAME), f32),
            pltpu.VMEM((256, FRAME), bf16),
            pltpu.VMEM((2 * CHANS, FRAME), bf16),
            pltpu.VMEM((4 * CHANS, LANES), f32),
            pltpu.VMEM((NZ, NY * NX, 4, LANES), bf16),
            pltpu.VMEM((NZ, NY * NX, 4, LANES), bf16),
            pltpu.VMEM((TAPS - 1, 4, FRAME), bf16),
            pltpu.VMEM((TAPS - 1, 4, FRAME), bf16),
            dma((7,)),
            dma((2,)),
            dma,
            dma((len(WAVES),)),
            dma((len(WAVES),)),
            dma((len(WAVES),)),
            pltpu.SemaphoreType.REGULAR((NZ,)),
            pltpu.SemaphoreType.REGULAR,
            pltpu.SemaphoreType.REGULAR,
        ],
        compiler_params=pltpu.CompilerParams(
            collective_id=0, has_side_effects=True, vmem_limit_bytes=VMEM_LIMIT
        ),
        name="channelize",
    )(*(pltpu.with_memory_space_constraint(a, pltpu.MemorySpace.HBM) for a in inputs))
    turned = turned.reshape(NX, NY, NZ, 16, LANES)
    return pl.pallas_call(
        correlate_kernel,
        out_shape=jax.ShapeDtypeStruct((1, 1, 2, 512, 512), f32),
        in_specs=[pl.BlockSpec(memory_space=pltpu.VMEM)],
        out_specs=hbm,
        scratch_shapes=[
            pltpu.VMEM((1, 1, 2, 512, 512), f32),
            dma((STEPS,)),
        ],
        compiler_params=pltpu.CompilerParams(vmem_limit_bytes=VMEM_LIMIT),
        name="correlate",
    )(turned)


def solution(mesh):
    placed = (P(("freq", "bl"), "tm", None), P())
    return jax.shard_map(
        on_device,
        mesh=mesh,
        in_specs=placed,
        out_specs=P(("freq", "tm"), "bl", None, None, None),
        check_vma=False,
    )
```

```python
import math

import jax
import jax.numpy as jnp
import numpy as np
from jax import lax
from jax.experimental import pallas as pl
from jax.experimental.pallas import tpu as pltpu
from jax.sharding import PartitionSpec as P

TAPS = 4
FRAME = 2048
NY, NZ, NX = 4, 16, 2
CHANS = NY * NZ * NX
LANES = 128
MESH = pl.DeviceIdType.MESH
OFFSETS = (0, 1, -1, 2, -2, 3, -3, 4, -4, 5, -5, 6, -6, 7, -7, 8)
WAVES = ((0, 7), (7, 11), (11, 15), (15, 16))
EARLY = NZ // 2
HUB_Z = 11
VMEM_LIMIT = 40 * 2**20
UNROLL = 4
STEPS = 4


def tap_constants():
    place = np.arange(TAPS * FRAME, dtype=np.float64) + 0.5
    shifted = (place - 2.0 * FRAME) / FRAME
    window = 0.5 - 0.5 * np.cos(place * (2.0 * math.pi / (TAPS * FRAME)))
    taps = (np.sinc(shifted) * window).reshape(TAPS, FRAME).astype(np.float32)
    return taps * np.float32(0.25)


def cos_sin(phase):
    turn = (phase + FRAME // 8) >> 9
    rest = (phase - (turn << 9)).astype(jnp.float32) * (2.0 * math.pi / FRAME)
    sq = rest * rest
    sin = rest * (1.0 + sq * (-1.0 / 6 + sq * (1.0 / 120 + sq * (-1.0 / 5040 + sq * (1.0 / 362880)))))
    cos = 1.0 + sq * (-0.5 + sq * (1.0 / 24 + sq * (-1.0 / 720 + sq * (1.0 / 40320))))
    odd = (turn & 1) == 1
    c = jnp.where(odd, sin, cos)
    s = jnp.where(odd, cos, sin)
    c = jnp.where(((turn + 1) & 2) == 2, -c, c)
    s = jnp.where((turn & 2) == 2, -s, s)
    return c, s


def taps_applied(ext, taps):
    prior = pltpu.roll(ext, 1, 0)
    early = taps[1:2] * ext + taps[0:1] * prior
    late = taps[3:4] * ext + taps[2:3] * prior
    return (late + pltpu.roll(early, 2, 0))[8:].astype(jnp.bfloat16)


def centred(samples):
    return samples.astype(jnp.float32) - 7.5


def make_table(chan_ref, table, lo, hi):
    rows = 16
    lane = lax.broadcasted_iota(jnp.int32, (rows, LANES), 1)
    scale = 1.0 / math.sqrt(FRAME)

    @pl.loop(lo, hi, unroll=2)
    def _(block):
        row = lax.broadcasted_iota(jnp.int32, (rows, LANES), 0) + block * rows
        source = ((row >> 1) & 3) * (NZ * NX) + (row >> 3) * NX + (row & 1)
        picked = jnp.where(lane == source, jnp.broadcast_to(chan_ref[...], (rows, LANES)), 0)
        chan = jnp.sum(picked.astype(jnp.float32), axis=1, keepdims=True)
        chan = jnp.broadcast_to(chan, (rows, LANES)).astype(jnp.int32)
        re, im = cos_sin((chan * lane) & (FRAME - 1))
        parts = [(re * scale, -im * scale)]
        for step in (128, 256):
            c, s = cos_sin((chan * step) & (FRAME - 1))
            parts += [(a * c + b * s, b * c - a * s) for a, b in parts]
        quarter = chan & 3
        c = jnp.where(quarter == 0, 1.0, jnp.where(quarter == 2, -1.0, 0.0))
        s = jnp.where(quarter == 1, 1.0, jnp.where(quarter == 3, -1.0, 0.0))
        parts += [(a * c + b * s, b * c - a * s) for a, b in parts]
        sign = (1 - 2 * (chan & 1)).astype(jnp.float32)
        parts += [(a * sign, b * sign) for a, b in parts]
        at = pl.multiple_of(block * rows, rows)
        for k, (a, b) in enumerate(parts):
            table[pl.ds(at, rows), k * LANES : (k + 1) * LANES] = a.astype(jnp.bfloat16)
            table[pl.ds(at + CHANS, rows), k * LANES : (k + 1) * LANES] = b.astype(jnp.bfloat16)


def channelize_kernel(
    samples, chan_hbm, taps_hbm, turned,
    raw, chan_ref, taps_ref, filtered, table, spread, mine, held, edge_out, edge_in,
    load_sem, edge_sem, zsend, zrecv, psend, precv, in_sem, plane_sem, late_sem,
):
    freq = lax.axis_index("freq")
    tm = lax.axis_index("tm")
    bl = lax.axis_index("bl")
    y, z = freq // NZ, freq % NZ
    half = y // 2

    barrier = pltpu.get_barrier_semaphore()
    partner = (freq, 1 - tm, bl)
    early = z < EARLY
    along_hub = z == HUB_Z
    plane_hub = (y == 2) & (tm == 1) & (bl == 0)
    hub = along_hub | plane_hub

    def signal(sem, device):
        pl.semaphore_signal(sem, inc=1, device_id=device, device_id_type=MESH)

    def along(t):
        return (y * NZ + t, tm, bl)

    signal(barrier, partner)

    loads = [
        pltpu.make_async_copy(samples.at[:, 56:64], raw.at[:, 56:64], load_sem.at[0]),
        pltpu.make_async_copy(chan_hbm, chan_ref, load_sem.at[5]),
        pltpu.make_async_copy(taps_hbm, taps_ref, load_sem.at[6]),
    ]
    for i in range(4):
        loads.append(pltpu.make_async_copy(samples.at[i, 0:56], raw.at[i, 0:56], load_sem.at[1 + i]))
    for copy in loads:
        copy.start()

    @pl.when(early)
    def _():
        @pl.loop(z + 1, NZ)
        def _(t):
            signal(barrier, along(t))

    @pl.when(jnp.logical_not(early | along_hub))
    def _():
        signal(barrier, along(HUB_Z))

    @pl.when(jnp.logical_not(plane_hub))
    def _():
        signal(barrier, (2 * NZ + z, 1, 0))

    contacts = jnp.where(early, z, jnp.where(along_hub, NZ - 1, EARLY))
    contacts += jnp.where(plane_hub, 32, 1)

    loads[0].wait()
    edge_copy = pltpu.make_async_remote_copy(
        edge_out, edge_in, edge_sem.at[0], edge_sem.at[1], device_id=partner, device_id_type=MESH
    )
    for f in range(TAPS - 1):
        last = [raw[i, 64 - (TAPS - 1) + f : 65 - (TAPS - 1) + f] for i in range(4)]
        edge_out[f] = centred(jnp.concatenate(last, axis=0)).astype(jnp.bfloat16)
    loads[1].wait()
    make_table(chan_ref, table, 0, 6)

    def plane_in():
        for n in range(31, 0, -1):
            signal(plane_sem, ((y + n // 8) % NY * NZ + z, (tm + n // 4) % NX, (bl + n) % 4))

    def pass_on():
        @pl.when(along_hub)
        def _():
            for t in range(EARLY, NZ):
                if t != HUB_Z:
                    signal(late_sem, along(t))

        @pl.when(plane_hub & early)
        def _():
            plane_in()

    def meet():
        pl.semaphore_wait(barrier, contacts)

        @pl.when(tm == 0)
        def _():
            edge_copy.start()

        @pl.loop(0, jnp.where(early, z, EARLY))
        def _(t):
            signal(in_sem.at[z], along(t))

        pass_on()

    @pl.when(jnp.logical_not(hub))
    def _():
        meet()

    make_table(chan_ref, table, 6, 8)
    loads[2].wait()

    for i in range(4):
        loads[3 + i].wait()

        @pl.loop(0, FRAME // LANES, unroll=UNROLL)
        def _(k):
            cols = pl.ds(pl.multiple_of(k * LANES, LANES), LANES)
            filtered[i * 64 + 8 : i * 64 + 64, cols] = taps_applied(centred(raw[i, :, cols]), taps_ref[:, cols])

    @pl.when(hub)
    def _():
        meet()

    @pl.when(tm == 0)
    def _():
        edge_in[...] = jnp.zeros_like(edge_in)
        edge_copy.wait_send()

    @pl.when(tm == 1)
    def _():
        edge_copy.wait_recv()

    @pl.loop(0, FRAME // LANES, unroll=2)
    def _(k):
        cols = pl.ds(pl.multiple_of(k * LANES, LANES), LANES)
        before = [edge_in[f, :, cols].astype(jnp.float32) for f in range(TAPS - 1)]
        for i in range(4):
            past = [before[f][i : i + 1] for f in (0, 0, 0, 0, 0, 0, 1, 2)]
            ext = jnp.concatenate(past + [centred(raw[i, 0:8, cols])], axis=0)
            filtered[i * 64 : i * 64 + 8, cols] = taps_applied(ext, taps_ref[:, cols])

    spectra = lax.dot_general(
        table[...], filtered[...], (((1,), (1,)), ((), ())), preferred_element_type=jnp.float32
    )
    first = lax.broadcasted_iota(jnp.int32, (CHANS, LANES), 1) < 64
    for t in range(2):
        re = spectra[:CHANS, t * LANES : (t + 1) * LANES]
        im = spectra[CHANS:, t * LANES : (t + 1) * LANES]
        spread[pl.ds(2 * t, CHANS, stride=4), :] = jnp.where(first, re, pltpu.roll(im, 64, 1))
        spread[pl.ds(2 * t + 1, CHANS, stride=4), :] = jnp.where(first, pltpu.roll(re, 64, 1), im)
    mine[...] = spread[...].astype(jnp.bfloat16).reshape(NZ, NY * NX, 4, LANES)

    def send_along(t):
        d = (z - t + 7 + NZ) % NZ - 7
        slot = jnp.where(d > 0, 2 * d - 1, -2 * d)
        wave = sum((slot >= lo).astype(jnp.int32) for lo, _ in WAVES[1:])
        pltpu.make_async_remote_copy(
            mine.at[t], held.at[slot], zsend, zrecv.at[wave], device_id=along(t), device_id_type=MESH
        ).start()

    pltpu.make_async_copy(mine.at[z], held.at[0], zrecv.at[0]).start()

    @pl.when(early)
    def _():
        @pl.loop(0, z)
        def _(t):
            send_along(t)

        @pl.loop(z + 1, NZ)
        def _(t):
            pl.semaphore_wait(in_sem.at[t], 1)
            send_along(t)

    @pl.when(jnp.logical_not(early))
    def _():
        @pl.loop(0, EARLY)
        def _(t):
            send_along(t)

        @pl.when(plane_hub)
        def _():
            plane_in()

        @pl.when(jnp.logical_not(along_hub))
        def _():
            pl.semaphore_wait(late_sem, 1)

        @pl.loop(EARLY, z)
        def _(t):
            send_along(t)

        @pl.loop(z + 1, NZ)
        def _(t):
            send_along(t)

    @pl.when(jnp.logical_not(plane_hub))
    def _():
        pl.semaphore_wait(plane_sem, 1)

    for w, (lo, hi) in enumerate(WAVES):
        pltpu.make_async_copy(held.at[lo:hi], held.at[lo:hi], zrecv.at[w]).wait()
        land = turned.at[tm, y, lo:hi, bl]
        for y_to in ((y + 2) % NY, (y + 1) % NY, (y + 3) % NY, y):
            for x_to in range(NX):
                block = held.at[lo:hi, y_to * NX + x_to]
                for to in (1, 3 * half, 2):
                    here = (y_to == y) & (x_to == tm) & (to == bl)

                    @pl.when(jnp.logical_not(here))
                    def _():
                        pltpu.make_async_remote_copy(
                            block, land, psend.at[w], precv.at[w],
                            device_id=(y_to * NZ + z, x_to, to), device_id_type=MESH,
                        ).start()

                    @pl.when(here)
                    def _():
                        pltpu.make_async_copy(block, land, precv.at[w]).start()

    middle = (bl == 1) | (bl == 2)
    to_self = middle | (bl == 3 * half)
    for w, (lo, hi) in enumerate(WAVES):

        @pl.when(to_self)
        def _():
            sent = spread.at[0 : 46 * (hi - lo)]
            pltpu.make_async_copy(sent, sent, psend.at[w]).wait()

        @pl.when(jnp.logical_not(to_self))
        def _():
            sent = spread.at[0 : 48 * (hi - lo)]
            pltpu.make_async_copy(sent, sent, psend.at[w]).wait()

        @pl.when(middle)
        def _():
            got = turned.at[:, :, lo:hi]
            pltpu.make_async_copy(got, got, precv.at[w]).wait()

        @pl.when(jnp.logical_not(middle))
        def _():
            got = turned.at[:, 0:2, lo:hi]
            pltpu.make_async_copy(got, got, precv.at[w]).wait()

    sent = mine.at[0 : NZ - 1]
    pltpu.make_async_copy(sent, sent, zsend).wait()


def correlate_kernel(turned, out, made, sems):
    z = lax.axis_index("freq") % NZ
    bl = lax.axis_index("bl")

    def rows(half, first, count):
        parts = []
        for n in range(first, first + count // 16):
            d = (n % NZ - z + 7 + NZ) % NZ - 7
            slot = jnp.where(d > 0, 2 * d - 1, -2 * d)
            parts.append([turned[x, half * 2 + n // NZ, slot] for x in range(NX)])
        return [jnp.concatenate(p, axis=0) for p in zip(*parts)]

    sign = jnp.where(lax.broadcasted_iota(jnp.int32, (1, LANES), 1) < 64, 1.0, -1.0)
    cols = jnp.concatenate(rows(bl % 2, 0, 512), axis=1)
    count = 512 // STEPS
    copies = []
    for step in range(STEPS):
        halves = rows(bl // 2, step * count // 16, count)
        turned_halves = [(pltpu.roll(h.astype(jnp.float32), 64, 1) * sign).astype(jnp.bfloat16) for h in halves]
        left = jnp.concatenate([jnp.concatenate(h, axis=1) for h in (halves, turned_halves)], axis=0)
        product = lax.dot_general(left, cols, (((1,), (1,)), ((), ())), preferred_element_type=jnp.float32)
        place = slice(step * count, (step + 1) * count)
        for p in range(2):
            made[0, 0, p, place] = product[p * count : (p + 1) * count] * (1.0 / 128)
        copies.append(pltpu.make_async_copy(made.at[:, :, :, place], out.at[:, :, :, place], sems.at[step]))
        copies[-1].start()
    for copy in copies:
        copy.wait()


def on_device(samples, chan_index):
    bf16, f32 = jnp.bfloat16, jnp.float32
    hbm = pl.BlockSpec(memory_space=pltpu.MemorySpace.HBM)
    dma = pltpu.SemaphoreType.DMA
    inputs = (samples, chan_index.reshape(1, CHANS), jnp.asarray(tap_constants()))
    turned = pl.pallas_call(
        channelize_kernel,
        out_shape=jax.ShapeDtypeStruct((NX, NY, NZ, 4, 4, LANES), bf16),
        in_specs=[hbm, hbm, hbm],
        out_specs=pl.BlockSpec(memory_space=pl.ANY),
        scratch_shapes=[
            pltpu.VMEM((4, 64, FRAME), jnp.int32),
            pltpu.VMEM((1, CHANS), jnp.int32),
            pltpu.VMEM((TAPS, FRAME), f32),
            pltpu.VMEM((256, FRAME), bf16),
            pltpu.VMEM((2 * CHANS, FRAME), bf16),
            pltpu.VMEM((4 * CHANS, LANES), f32),
            pltpu.VMEM((NZ, NY * NX, 4, LANES), bf16),
            pltpu.VMEM((NZ, NY * NX, 4, LANES), bf16),
            pltpu.VMEM((TAPS - 1, 4, FRAME), bf16),
            pltpu.VMEM((TAPS - 1, 4, FRAME), bf16),
            dma((7,)),
            dma((2,)),
            dma,
            dma((len(WAVES),)),
            dma((len(WAVES),)),
            dma((len(WAVES),)),
            pltpu.SemaphoreType.REGULAR((NZ,)),
            pltpu.SemaphoreType.REGULAR,
            pltpu.SemaphoreType.REGULAR,
        ],
        compiler_params=pltpu.CompilerParams(
            collective_id=0, has_side_effects=True, vmem_limit_bytes=VMEM_LIMIT
        ),
        name="channelize",
    )(*(pltpu.with_memory_space_constraint(a, pltpu.MemorySpace.HBM) for a in inputs))
    turned = turned.reshape(NX, NY, NZ, 16, LANES)
    return pl.pallas_call(
        correlate_kernel,
        out_shape=jax.ShapeDtypeStruct((1, 1, 2, 512, 512), f32),
        in_specs=[pl.BlockSpec(memory_space=pltpu.VMEM)],
        out_specs=hbm,
        scratch_shapes=[
            pltpu.VMEM((1, 1, 2, 512, 512), f32),
            dma((STEPS,)),
        ],
        compiler_params=pltpu.CompilerParams(vmem_limit_bytes=VMEM_LIMIT),
        name="correlate",
    )(turned)


def solution(mesh):
    placed = (P(("freq", "bl"), "tm", None), P())
    return jax.shard_map(
        on_device,
        mesh=mesh,
        in_specs=placed,
        out_specs=P(("freq", "tm"), "bl", None, None, None),
        check_vma=False,
    )
```

```python
import math

import jax
import jax.numpy as jnp
import numpy as np
from jax import lax
from jax.experimental import pallas as pl
from jax.experimental.pallas import tpu as pltpu
from jax.sharding import PartitionSpec as P

TAPS = 4
FRAME = 2048
NY, NZ, NX = 4, 16, 2
CHANS = NY * NZ * NX
LANES = 128
MESH = pl.DeviceIdType.MESH
OFFSETS = (0, 1, -1, 2, -2, 3, -3, 4, -4, 5, -5, 6, -6, 7, -7, 8)
WAVES = ((0, 9), (9, 15), (15, 16))
EARLY = NZ // 2
HUB_Z = 11
VMEM_LIMIT = 40 * 2**20
UNROLL = 4
STEPS = 4


def tap_constants():
    place = np.arange(TAPS * FRAME, dtype=np.float64) + 0.5
    shifted = (place - 2.0 * FRAME) / FRAME
    window = 0.5 - 0.5 * np.cos(place * (2.0 * math.pi / (TAPS * FRAME)))
    taps = (np.sinc(shifted) * window).reshape(TAPS, FRAME).astype(np.float32)
    return taps * np.float32(0.25)


def cos_sin(phase):
    turn = (phase + FRAME // 8) >> 9
    rest = (phase - (turn << 9)).astype(jnp.float32) * (2.0 * math.pi / FRAME)
    sq = rest * rest
    sin = rest * (1.0 + sq * (-1.0 / 6 + sq * (1.0 / 120 + sq * (-1.0 / 5040 + sq * (1.0 / 362880)))))
    cos = 1.0 + sq * (-0.5 + sq * (1.0 / 24 + sq * (-1.0 / 720 + sq * (1.0 / 40320))))
    odd = (turn & 1) == 1
    c = jnp.where(odd, sin, cos)
    s = jnp.where(odd, cos, sin)
    c = jnp.where(((turn + 1) & 2) == 2, -c, c)
    s = jnp.where((turn & 2) == 2, -s, s)
    return c, s


def taps_applied(ext, taps):
    prior = pltpu.roll(ext, 1, 0)
    early = taps[1:2] * ext + taps[0:1] * prior
    late = taps[3:4] * ext + taps[2:3] * prior
    return (late + pltpu.roll(early, 2, 0))[8:].astype(jnp.bfloat16)


def centred(samples):
    return samples.astype(jnp.float32) - 7.5


def make_table(chan_ref, table, lo, hi):
    rows = 16
    lane = lax.broadcasted_iota(jnp.int32, (rows, LANES), 1)
    scale = 1.0 / math.sqrt(FRAME)

    @pl.loop(lo, hi, unroll=2)
    def _(block):
        row = lax.broadcasted_iota(jnp.int32, (rows, LANES), 0) + block * rows
        source = ((row >> 1) & 3) * (NZ * NX) + (row >> 3) * NX + (row & 1)
        picked = jnp.where(lane == source, jnp.broadcast_to(chan_ref[...], (rows, LANES)), 0)
        chan = jnp.sum(picked.astype(jnp.float32), axis=1, keepdims=True)
        chan = jnp.broadcast_to(chan, (rows, LANES)).astype(jnp.int32)
        re, im = cos_sin((chan * lane) & (FRAME - 1))
        parts = [(re * scale, -im * scale)]
        for step in (128, 256):
            c, s = cos_sin((chan * step) & (FRAME - 1))
            parts += [(a * c + b * s, b * c - a * s) for a, b in parts]
        quarter = chan & 3
        c = jnp.where(quarter == 0, 1.0, jnp.where(quarter == 2, -1.0, 0.0))
        s = jnp.where(quarter == 1, 1.0, jnp.where(quarter == 3, -1.0, 0.0))
        parts += [(a * c + b * s, b * c - a * s) for a, b in parts]
        sign = (1 - 2 * (chan & 1)).astype(jnp.float32)
        parts += [(a * sign, b * sign) for a, b in parts]
        at = pl.multiple_of(block * rows, rows)
        for k, (a, b) in enumerate(parts):
            table[pl.ds(at, rows), k * LANES : (k + 1) * LANES] = a.astype(jnp.bfloat16)
            table[pl.ds(at + CHANS, rows), k * LANES : (k + 1) * LANES] = b.astype(jnp.bfloat16)


def channelize_kernel(
    samples, chan_hbm, taps_hbm, turned,
    raw, chan_ref, taps_ref, filtered, table, spread, mine, held, edge_out, edge_in,
    load_sem, edge_sem, zsend, zrecv, psend, precv, in_sem, plane_sem, late_sem,
):
    freq = lax.axis_index("freq")
    tm = lax.axis_index("tm")
    bl = lax.axis_index("bl")
    y, z = freq // NZ, freq % NZ
    half = y // 2

    barrier = pltpu.get_barrier_semaphore()
    partner = (freq, 1 - tm, bl)
    early = z < EARLY
    along_hub = z == HUB_Z
    plane_hub = (y == 2) & (tm == 1) & (bl == 0)
    hub = along_hub | plane_hub

    def signal(sem, device):
        pl.semaphore_signal(sem, inc=1, device_id=device, device_id_type=MESH)

    def along(t):
        return (y * NZ + t, tm, bl)

    signal(barrier, partner)

    loads = [
        pltpu.make_async_copy(samples.at[:, 56:64], raw.at[:, 56:64], load_sem.at[0]),
        pltpu.make_async_copy(chan_hbm, chan_ref, load_sem.at[5]),
        pltpu.make_async_copy(taps_hbm, taps_ref, load_sem.at[6]),
    ]
    for i in range(4):
        loads.append(pltpu.make_async_copy(samples.at[i, 0:56], raw.at[i, 0:56], load_sem.at[1 + i]))
    for copy in loads:
        copy.start()

    @pl.when(early)
    def _():
        @pl.loop(z + 1, NZ)
        def _(t):
            signal(barrier, along(t))

    @pl.when(jnp.logical_not(early | along_hub))
    def _():
        signal(barrier, along(HUB_Z))

    @pl.when(jnp.logical_not(plane_hub))
    def _():
        signal(barrier, (2 * NZ + z, 1, 0))

    contacts = jnp.where(early, z, jnp.where(along_hub, NZ - 1, EARLY))
    contacts += jnp.where(plane_hub, 32, 1)

    loads[0].wait()
    edge_copy = pltpu.make_async_remote_copy(
        edge_out, edge_in, edge_sem.at[0], edge_sem.at[1], device_id=partner, device_id_type=MESH
    )
    for f in range(TAPS - 1):
        last = [raw[i, 64 - (TAPS - 1) + f : 65 - (TAPS - 1) + f] for i in range(4)]
        edge_out[f] = centred(jnp.concatenate(last, axis=0)).astype(jnp.bfloat16)
    loads[1].wait()
    make_table(chan_ref, table, 0, 6)

    def plane_in():
        for n in range(31, 0, -1):
            signal(plane_sem, ((y + n // 8) % NY * NZ + z, (tm + n // 4) % NX, (bl + n) % 4))

    def pass_on():
        @pl.when(along_hub)
        def _():
            for t in range(EARLY, NZ):
                if t != HUB_Z:
                    signal(late_sem, along(t))

        @pl.when(plane_hub & early)
        def _():
            plane_in()

    def meet():
        pl.semaphore_wait(barrier, contacts)

        @pl.when(tm == 0)
        def _():
            edge_copy.start()

        @pl.loop(0, jnp.where(early, z, EARLY))
        def _(t):
            signal(in_sem.at[z], along(t))

        pass_on()

    @pl.when(jnp.logical_not(hub))
    def _():
        meet()

    make_table(chan_ref, table, 6, 8)
    loads[2].wait()

    for i in range(4):
        loads[3 + i].wait()

        @pl.loop(0, FRAME // LANES, unroll=UNROLL)
        def _(k):
            cols = pl.ds(pl.multiple_of(k * LANES, LANES), LANES)
            filtered[i * 64 + 8 : i * 64 + 64, cols] = taps_applied(centred(raw[i, :, cols]), taps_ref[:, cols])

    @pl.when(hub)
    def _():
        meet()

    @pl.when(tm == 0)
    def _():
        edge_in[...] = jnp.zeros_like(edge_in)
        edge_copy.wait_send()

    @pl.when(tm == 1)
    def _():
        edge_copy.wait_recv()

    @pl.loop(0, FRAME // LANES, unroll=2)
    def _(k):
        cols = pl.ds(pl.multiple_of(k * LANES, LANES), LANES)
        before = [edge_in[f, :, cols].astype(jnp.float32) for f in range(TAPS - 1)]
        for i in range(4):
            past = [before[f][i : i + 1] for f in (0, 0, 0, 0, 0, 0, 1, 2)]
            ext = jnp.concatenate(past + [centred(raw[i, 0:8, cols])], axis=0)
            filtered[i * 64 : i * 64 + 8, cols] = taps_applied(ext, taps_ref[:, cols])

    spectra = lax.dot_general(
        table[...], filtered[...], (((1,), (1,)), ((), ())), preferred_element_type=jnp.float32
    )
    first = lax.broadcasted_iota(jnp.int32, (CHANS, LANES), 1) < 64
    for t in range(2):
        re = spectra[:CHANS, t * LANES : (t + 1) * LANES]
        im = spectra[CHANS:, t * LANES : (t + 1) * LANES]
        spread[pl.ds(2 * t, CHANS, stride=4), :] = jnp.where(first, re, pltpu.roll(im, 64, 1))
        spread[pl.ds(2 * t + 1, CHANS, stride=4), :] = jnp.where(first, pltpu.roll(re, 64, 1), im)
    mine[...] = spread[...].astype(jnp.bfloat16).reshape(NZ, NY * NX, 4, LANES)

    def send_along(t):
        d = (z - t + 7 + NZ) % NZ - 7
        slot = jnp.where(d > 0, 2 * d - 1, -2 * d)
        wave = sum((slot >= lo).astype(jnp.int32) for lo, _ in WAVES[1:])
        pltpu.make_async_remote_copy(
            mine.at[t], held.at[slot], zsend, zrecv.at[wave], device_id=along(t), device_id_type=MESH
        ).start()

    pltpu.make_async_copy(mine.at[z], held.at[0], zrecv.at[0]).start()

    @pl.when(early)
    def _():
        @pl.loop(0, z)
        def _(t):
            send_along(t)

        @pl.loop(z + 1, NZ)
        def _(t):
            pl.semaphore_wait(in_sem.at[t], 1)
            send_along(t)

    @pl.when(jnp.logical_not(early))
    def _():
        @pl.loop(0, EARLY)
        def _(t):
            send_along(t)

        @pl.when(plane_hub)
        def _():
            plane_in()

        @pl.when(jnp.logical_not(along_hub))
        def _():
            pl.semaphore_wait(late_sem, 1)

        @pl.loop(EARLY, z)
        def _(t):
            send_along(t)

        @pl.loop(z + 1, NZ)
        def _(t):
            send_along(t)

    @pl.when(jnp.logical_not(plane_hub))
    def _():
        pl.semaphore_wait(plane_sem, 1)

    for w, (lo, hi) in enumerate(WAVES):
        pltpu.make_async_copy(held.at[lo:hi], held.at[lo:hi], zrecv.at[w]).wait()
        land = turned.at[tm, y, lo:hi, bl]
        for y_to in ((y + 2) % NY, (y + 1) % NY, (y + 3) % NY, y):
            for x_to in range(NX):
                block = held.at[lo:hi, y_to * NX + x_to]
                for to in (1, 3 * half, 2):
                    here = (y_to == y) & (x_to == tm) & (to == bl)

                    @pl.when(jnp.logical_not(here))
                    def _():
                        pltpu.make_async_remote_copy(
                            block, land, psend.at[w], precv.at[w],
                            device_id=(y_to * NZ + z, x_to, to), device_id_type=MESH,
                        ).start()

                    @pl.when(here)
                    def _():
                        pltpu.make_async_copy(block, land, precv.at[w]).start()

    middle = (bl == 1) | (bl == 2)
    to_self = middle | (bl == 3 * half)
    for w, (lo, hi) in enumerate(WAVES):

        @pl.when(to_self)
        def _():
            sent = spread.at[0 : 46 * (hi - lo)]
            pltpu.make_async_copy(sent, sent, psend.at[w]).wait()

        @pl.when(jnp.logical_not(to_self))
        def _():
            sent = spread.at[0 : 48 * (hi - lo)]
            pltpu.make_async_copy(sent, sent, psend.at[w]).wait()

        @pl.when(middle)
        def _():
            got = turned.at[:, :, lo:hi]
            pltpu.make_async_copy(got, got, precv.at[w]).wait()

        @pl.when(jnp.logical_not(middle))
        def _():
            got = turned.at[:, 0:2, lo:hi]
            pltpu.make_async_copy(got, got, precv.at[w]).wait()

    sent = mine.at[0 : NZ - 1]
    pltpu.make_async_copy(sent, sent, zsend).wait()


def correlate_kernel(turned, out, made, sems):
    z = lax.axis_index("freq") % NZ
    bl = lax.axis_index("bl")

    def rows(half, first, count):
        parts = []
        for n in range(first, first + count // 16):
            d = (n % NZ - z + 7 + NZ) % NZ - 7
            slot = jnp.where(d > 0, 2 * d - 1, -2 * d)
            parts.append([turned[x, half * 2 + n // NZ, slot] for x in range(NX)])
        return [jnp.concatenate(p, axis=0) for p in zip(*parts)]

    sign = jnp.where(lax.broadcasted_iota(jnp.int32, (1, LANES), 1) < 64, 1.0, -1.0)
    cols = jnp.concatenate(rows(bl % 2, 0, 512), axis=1)
    count = 512 // STEPS
    copies = []
    for step in range(STEPS):
        halves = rows(bl // 2, step * count // 16, count)
        turned_halves = [(pltpu.roll(h.astype(jnp.float32), 64, 1) * sign).astype(jnp.bfloat16) for h in halves]
        left = jnp.concatenate([jnp.concatenate(h, axis=1) for h in (halves, turned_halves)], axis=0)
        product = lax.dot_general(left, cols, (((1,), (1,)), ((), ())), preferred_element_type=jnp.float32)
        place = slice(step * count, (step + 1) * count)
        for p in range(2):
            made[0, 0, p, place] = product[p * count : (p + 1) * count] * (1.0 / 128)
        copies.append(pltpu.make_async_copy(made.at[:, :, :, place], out.at[:, :, :, place], sems.at[step]))
        copies[-1].start()
    for copy in copies:
        copy.wait()


def on_device(samples, chan_index):
    bf16, f32 = jnp.bfloat16, jnp.float32
    hbm = pl.BlockSpec(memory_space=pltpu.MemorySpace.HBM)
    dma = pltpu.SemaphoreType.DMA
    inputs = (samples, chan_index.reshape(1, CHANS), jnp.asarray(tap_constants()))
    turned = pl.pallas_call(
        channelize_kernel,
        out_shape=jax.ShapeDtypeStruct((NX, NY, NZ, 4, 4, LANES), bf16),
        in_specs=[hbm, hbm, hbm],
        out_specs=pl.BlockSpec(memory_space=pl.ANY),
        scratch_shapes=[
            pltpu.VMEM((4, 64, FRAME), jnp.int32),
            pltpu.VMEM((1, CHANS), jnp.int32),
            pltpu.VMEM((TAPS, FRAME), f32),
            pltpu.VMEM((256, FRAME), bf16),
            pltpu.VMEM((2 * CHANS, FRAME), bf16),
            pltpu.VMEM((4 * CHANS, LANES), f32),
            pltpu.VMEM((NZ, NY * NX, 4, LANES), bf16),
            pltpu.VMEM((NZ, NY * NX, 4, LANES), bf16),
            pltpu.VMEM((TAPS - 1, 4, FRAME), bf16),
            pltpu.VMEM((TAPS - 1, 4, FRAME), bf16),
            dma((7,)),
            dma((2,)),
            dma,
            dma((len(WAVES),)),
            dma((len(WAVES),)),
            dma((len(WAVES),)),
            pltpu.SemaphoreType.REGULAR((NZ,)),
            pltpu.SemaphoreType.REGULAR,
            pltpu.SemaphoreType.REGULAR,
        ],
        compiler_params=pltpu.CompilerParams(
            collective_id=0, has_side_effects=True, vmem_limit_bytes=VMEM_LIMIT
        ),
        name="channelize",
    )(*(pltpu.with_memory_space_constraint(a, pltpu.MemorySpace.HBM) for a in inputs))
    turned = turned.reshape(NX, NY, NZ, 16, LANES)
    return pl.pallas_call(
        correlate_kernel,
        out_shape=jax.ShapeDtypeStruct((1, 1, 2, 512, 512), f32),
        in_specs=[pl.BlockSpec(memory_space=pltpu.VMEM)],
        out_specs=hbm,
        scratch_shapes=[
            pltpu.VMEM((1, 1, 2, 512, 512), f32),
            dma((STEPS,)),
        ],
        compiler_params=pltpu.CompilerParams(vmem_limit_bytes=VMEM_LIMIT),
        name="correlate",
    )(turned)


def solution(mesh):
    placed = (P(("freq", "bl"), "tm", None), P())
    return jax.shard_map(
        on_device,
        mesh=mesh,
        in_specs=placed,
        out_specs=P(("freq", "tm"), "bl", None, None, None),
        check_vma=False,
    )
```
